32 devices in a mesh: img: 4 (over y, x), freq: 8 (over z, core).
Axes of the slice: x: 2, y: 2, z: 4, core: 2. Of those that a mesh axis runs over, the one named last changes fastest.
Arguments:
- images: bfloat16 [2, 6144, 32768], P(None, 'img', 'freq'), may hold values from -6 to 6
- references: bfloat16 [2, 896, 32768], P(None, 'img', 'freq'), may hold values from -6 to 6
- noise_weight: float32 [32768], P('freq'), may hold values from 0.005 to 0.05
- prior_orient: int32 [6144], P('img'), may hold values from 0 to 895
- segment_brick: int32 [8, 896, 32, 1], P('freq', 'img'), may hold values from 0 to 31; in each aligned block of 7168 rows (0 to 7167, 7168 to 14335, ..., all dimensions but the last counted through in order) at most 560 rows name the same one
- segment_row: int32 [8, 896, 32], P('freq', 'img'), may hold values from 0 to 1999
- segment_kernel: int32 [8, 896, 32], P('freq', 'img'), may hold values from 0 to 7
- kernel_taps: float32 [8, 4], replicated, may hold values from 0.1 to 1
Outputs:
- posterior: float32 [896, 6144], P('freq', 'img')
- volume: float32 [32, 2, 2000, 128], P(('img', 'freq'))
The draws below stay inside these ranges and needn't reach their ends.
Inputs may be any that keep to these rules, and one draw needn't show every extreme that they name: `segment_brick`: counted in aligned blocks of 7168 segments in the map's order, no brick is named more than 560 times within one block, a bound that some block reaches.
All inputs are finite; a program needn't handle non-finite values.
Results may differ from the reference program's by a relative error of at most 0.014.
Values may be sent and summed in bfloat16 or wider, within the bound.
No kernel may reach another device: no remote copies, remote signals or barrier semaphores. Data moves between devices by JAX's collectives and lax.ppermute only.
A program may use at most 128 MiB of HBM per device.

```python
import math
import jax
import jax.numpy as jnp
import numpy as np
from jax import lax

F = 32768
ORI = 896
SEG = 128
TAPS = 4
NKER = 8
IMG_DEV = 1536
BROWS = 2000
NIMG = 6144
SEGQ = 32
SEG_DEV = 7168
BRICKS = 32
CAP = 560
N_IMG = 4
N_FREQ = 8


def previous_orient(key):
    return jax.random.randint(jax.random.fold_in(key, 11), (NIMG,), 0, ORI, dtype=jnp.int32)


def drawn_references(key):
    return jnp.clip(jax.random.normal(jax.random.fold_in(key, 23), (2, ORI, F), jnp.float32), -6.0, 6.0)


def draw_references(key, part):
    sampled = drawn_references(key)
    return sampled.astype(jnp.bfloat16)


def draw_images(key, part):
    sampled = jnp.clip(jax.random.normal(jax.random.fold_in(key, 41), (2, NIMG, F), jnp.float32), -6.0, 6.0)
    return sampled.astype(jnp.bfloat16)


def draw_prior_orient(key, part):
    return previous_orient(key)


def place_ends(entries, key, low, high):
    longest = entries.shape.index(max(entries.shape))
    spots = []
    for shift in (0, 1):
        where = [jax.random.randint(jax.random.fold_in(key, axis), (), 0, length) for axis, length in enumerate(entries.shape)]
        where[longest] = (where[longest] + shift) % entries.shape[longest]
        spots.append(tuple(where))
    return entries.at[spots[0]].set(low).at[spots[1]].set(high)


def shard_levels(rng, dims, cuts, smallest, largest):
    def one(dim, shards_of):
        heights = jax.random.uniform(jax.random.fold_in(jax.random.fold_in(rng, 6), dim), (shards_of,), jnp.float32, smallest / len(cuts), largest / len(cuts))
        return jnp.repeat(jnp.exp(heights), dims[dim] // shards_of).reshape((-1,) + (1,) * (len(dims) - dim - 1))

    loudness = one(*cuts[0])
    for cut in cuts[1:]:
        loudness = loudness * one(*cut)
    return loudness


def assign_block(stream_key, own, number, rows, number_of, top, bound, lean):
    sequence = jax.random.permutation(stream_key, number_of)
    heavy_load, common = shares(number_of, rows * top, bound, lean, True), shares(number_of, rows * top, bound, lean, False)
    places = jnp.arange(number_of)

    def named(tallies, rotation):
        used = int((tallies > 0).sum())
        fixed = max(1, used // 4)
        passed = fixed + (places - fixed + rotation * (used - fixed)) % max(1, number_of - fixed)
        return jnp.zeros((number_of,), jnp.int32).at[sequence[jnp.where(places < fixed, places, passed)]].set(jnp.asarray(tallies, jnp.int32))

    tallies = jnp.where(number % 4 == 0, named(heavy_load, number // 4), named(common, number - number // 4 - 1))
    mixed = jax.random.permutation(jax.random.fold_in(own, 3), number_of)
    giver, taker = mixed[0:number_of // 2 * 2:2], mixed[1:number_of // 2 * 2:2]
    slack = jnp.minimum(tallies[giver] - 1, bound - tallies[taker]) // 2
    slack = jnp.where((giver == sequence[0]) | (taker == sequence[0]) | (tallies[taker] == 0), 0, jnp.maximum(slack, 0))
    passed = jax.random.randint(jax.random.fold_in(own, 4), (number_of // 2,), 0, 1 << 20) % (slack + 1)
    tallies = tallies.at[giver].add(-passed).at[taker].add(passed)
    members = jnp.searchsorted(jnp.cumsum(tallies), jnp.arange(rows * top), side="right").astype(jnp.int32)
    table = members.reshape(top, rows).T
    table = table[jax.random.permutation(jax.random.fold_in(own, 1), rows)]
    rotation = jax.random.randint(jax.random.fold_in(own, 2), (rows, 1), 0, top)
    return jnp.take_along_axis(table, (jnp.arange(top)[None, :] + rotation) % top, axis=1)


def shares(number_of, total, limit, lean, full):
    loads = [(1 << 20) // math.isqrt(grade ** lean) + 1 for grade in range(1, number_of + 1)]
    largest = limit if full else min(limit, max(-(-total // number_of), total * loads[0] // sum(loads)))
    least = 1 if total - largest >= number_of - 1 else 0
    holding, rest = [largest] + [least] * (number_of - 1), total - largest - least * (number_of - 1)
    while rest > 0:
        free = [i for i in range(1, number_of) if holding[i] < largest] or [i for i in range(1, number_of) if holding[i] < limit]
        mass, remaining = sum([loads[i] for i in free]), rest
        for i in free:
            more = min(limit - holding[i], max(1, remaining * loads[i] // mass), rest)
            holding[i] = holding[i] + more
            rest = rest - more
    return np.array(holding)


def setup_inputs(seed: int = 0) -> dict:
    splits = jax.random.split(jax.random.key(seed), 9)
    images = draw_images(jax.random.fold_in(splits[8], 71), 0)
    references = draw_references(jax.random.fold_in(splits[8], 71), 0)
    noise_weight = jnp.clip(jnp.exp(math.log(0.05) - 2.3025851 * jax.random.uniform(splits[2], (F,), jnp.float32) ** shard_levels(splits[2], (F,), ((0, 8),), -0.2, 0.2)), 0.005, 0.05)
    prior_orient = draw_prior_orient(jax.random.fold_in(splits[8], 71), 0)
    segment_brick_keys = jax.random.split(jax.random.fold_in(splits[4], 1), N_FREQ * ORI * SEGQ // SEG_DEV)
    segment_brick_turns = jax.random.permutation(jax.random.fold_in(splits[4], 3), N_FREQ * ORI * SEGQ // SEG_DEV)
    segment_brick = jax.vmap(lambda own, number: assign_block(jax.random.fold_in(splits[4], 2), own, number, SEG_DEV, BRICKS, 1, CAP, 1))(segment_brick_keys, segment_brick_turns).reshape((N_FREQ, ORI, SEGQ, 1))
    segment_row = place_ends(jax.random.randint(splits[5], (N_FREQ, ORI, SEGQ), 0, BROWS), jax.random.fold_in(splits[5], 1), 0, BROWS - 1).astype(jnp.int32)
    segment_kernel = place_ends(jax.random.randint(splits[6], (N_FREQ, ORI, SEGQ), 0, NKER), jax.random.fold_in(splits[6], 1), 0, NKER - 1).astype(jnp.int32)
    kernel_taps = jnp.clip(jax.random.uniform(splits[7], (NKER, TAPS), jnp.float32, 0.1, 1.0), 0.1, 1.0)
    return {"images": images, "references": references, "noise_weight": noise_weight, "prior_orient": prior_orient, "segment_brick": segment_brick, "segment_row": segment_row, "segment_kernel": segment_kernel, "kernel_taps": kernel_taps}


tempering = 0.5
masked_logit = -1.0e30
contract_last = (((1,), (1,)), ((), ()))


def spread_taps(values, kernels, kernel_taps):
    phases = kernel_taps.shape[0]
    tap_count = kernel_taps.shape[1]
    member = (kernels[:, None] == jnp.arange(phases, dtype=jnp.int32)[None, :]).astype(kernel_taps.dtype)
    factors = jnp.dot(member, kernel_taps, precision=lax.Precision.HIGHEST)
    padded = jnp.pad(values, ((0, 0), (0, 0), (tap_count - 2, 1)))
    lane_count = values.shape[2]
    result = jnp.zeros(values.shape, values.dtype)
    for tap_index in range(tap_count):
        first_lane = tap_count - 1 - tap_index
        result = result + factors[:, tap_index, None, None] * padded[:, :, first_lane:first_lane + lane_count]
    return result


def window_logits(scores, orient_index, prior_orient, orient_count):
    distance = (orient_index[:, None] - prior_orient[None, :]) % orient_count
    half_window = orient_count // 8
    allowed = (distance <= half_window) | (distance >= orient_count - half_window)
    return jnp.where(allowed, tempering * scores, masked_logit)


def reference(images, references, noise_weight, prior_orient, segment_brick, segment_row, segment_kernel, kernel_taps):
    unpacked = references.astype(jnp.float32)
    weighted = (noise_weight * unpacked).astype(jnp.bfloat16)
    energies = jnp.sum(noise_weight * (unpacked[0] * unpacked[0] + unpacked[1] * unpacked[1]), axis=1)
    products = lax.dot_general(weighted[0], images[0], contract_last, preferred_element_type=jnp.float32)
    products = products + lax.dot_general(weighted[1], images[1], contract_last, preferred_element_type=jnp.float32)
    scores = products - 0.5 * energies[:, None]
    orient_index = jnp.arange(ORI, dtype=jnp.int32)
    logits = window_logits(scores, orient_index, prior_orient, ORI)
    highest = jnp.max(logits, axis=0)
    raised = jnp.exp(logits - highest[None, :])
    posterior = raised / jnp.sum(raised, axis=0)[None, :]
    rounded = posterior.astype(jnp.bfloat16)

    def add_group(group_index, running):
        first_image = jnp.asarray(group_index, jnp.int32) * IMG_DEV
        weights = lax.dynamic_slice_in_dim(rounded, first_image, IMG_DEV, 1)
        image_block = lax.dynamic_slice_in_dim(images, first_image, IMG_DEV, 1)
        partial_value = jnp.stack((jnp.dot(weights, image_block[0], preferred_element_type=jnp.float32),
                             jnp.dot(weights, image_block[1], preferred_element_type=jnp.float32)), axis=1)
        narrowed = lax.optimization_barrier(partial_value.astype(jnp.bfloat16))
        return running + narrowed.astype(jnp.float32)

    weighted_sums = lax.fori_loop(0, N_IMG, add_group, jnp.zeros((ORI, 2, F), jnp.float32))
    segment_blocks = F // N_FREQ // SEG
    values = weighted_sums.reshape(ORI, 2, N_FREQ, segment_blocks, SEG).transpose(2, 0, 3, 1, 4).reshape(-1, 2, SEG)
    contributions = spread_taps(values, segment_kernel.reshape(-1), kernel_taps)
    places = segment_brick.reshape(-1) * BROWS + segment_row.reshape(-1)
    volume = jnp.zeros((BRICKS * BROWS, 2, SEG), jnp.float32).at[places].add(contributions)
    volume = volume.reshape(BRICKS, BROWS, 2, SEG).transpose(0, 2, 1, 3)
    return posterior, volume
```

```python
import functools

import jax
import jax.numpy as jnp
from jax import lax
from jax.experimental import pallas as pl
from jax.experimental.pallas import tpu as pltpu
from jax.sharding import PartitionSpec as P

BROWS = 2000
LANES = 128

tempering = 0.5
contract_last = (((1,), (1,)), ((), ()))
VMEM_BYTES = 60 * 1024 * 1024


def round_up(value, multiple):
    return -(-value // multiple) * multiple


def window_start(prior, half_window, orient_count):
    start = prior - half_window
    return jnp.where(start < 0, start + orient_count, start)


def bits_of(count):
    bit = 1
    while bit < count:
        yield bit
        bit *= 2


def cut_windows(half_window, prior_ref, score_ref, out_ref):
    orient_count = score_ref.shape[0]
    keep = out_ref.shape[0]
    for lanes in range(0, out_ref.shape[1], LANES):
        cols = slice(lanes, lanes + LANES)
        start = window_start(prior_ref[:, cols], half_window, orient_count)
        x = score_ref[:, cols]
        for bit in reversed(list(bits_of(orient_count))):
            kept = min(orient_count, round_up(bit - 1 + keep, 8))
            if bit >= 8:
                moved = jnp.concatenate([x[bit:], x[:bit]], axis=0)
            else:
                moved = pltpu.roll(x, x.shape[0] - bit, axis=0)
            x = jnp.where((start & bit) != 0, moved[:kept], x[:kept])
        out_ref[:, cols] = x


def cut_kernel(half_window, prior_ref, score_ref, out_ref):
    cut_windows(half_window, prior_ref, score_ref, out_ref)


def tail_kernel(half_window, own_ref, prior_ref, b0_ref, b1_ref, b2_ref, b3_ref, image_ref,
                w_first_ref, w_second_ref, out_ref, score_ref):
    block = b0_ref.shape[0]
    part = w_first_ref.shape[0]
    own = own_ref[0]

    def rows_of(relative):
        return pl.multiple_of((own ^ relative) * block, 8)

    for relative, ref in enumerate((b0_ref, b1_ref, b2_ref)):
        score_ref[pl.ds(rows_of(relative), block), :] = ref[...]
    image = image_ref[...]
    for index, ref in enumerate((w_first_ref, w_second_ref)):
        here = pl.ds(pl.multiple_of(rows_of(3) + index * part, 8), part)
        score_ref[here, :] = b3_ref[index * part : (index + 1) * part, :] + lax.dot_general(
            ref[...], image, contract_last, preferred_element_type=jnp.float32
        )
    cut_windows(half_window, prior_ref, score_ref, out_ref)


def spread_kernel(half_window, order, own_ref, prior_ref, score_ref, full_ref, share_ref, wide_ref):
    orient_count = wide_ref.shape[0]
    width = 2 * half_window + 1
    own, share = own_ref[0], own_ref[1]
    for lanes in range(0, score_ref.shape[1], LANES):
        cols = slice(lanes, lanes + LANES)
        start = window_start(prior_ref[:, cols], half_window, orient_count)
        scores = score_ref[:, cols]
        place = lax.broadcasted_iota(jnp.int32, scores.shape, 0)
        logits = jnp.where(place < width, tempering * scores, -1e30)
        highest = jnp.max(logits, axis=0, keepdims=True)
        raised = jnp.exp(logits - highest)
        x = raised / jnp.sum(raised, axis=0, keepdims=True)
        for bit in bits_of(orient_count):
            grown = min(orient_count, round_up(x.shape[0] + bit, 8))
            extra = grown - x.shape[0]
            if extra:
                x = jnp.concatenate([x, jnp.zeros((extra, LANES), x.dtype)], axis=0)
            if bit >= 8:
                moved = jnp.concatenate([x[-bit:], x[:-bit]], axis=0)
            else:
                moved = pltpu.roll(x, bit, axis=0)
            x = jnp.where((start & bit) != 0, moved, x)
        wide_ref[:, cols] = x
    if order is None:
        full_ref[...] = wide_ref[...].astype(full_ref.dtype)
    else:
        block = orient_count // len(order)
        for index, relative in enumerate(order):
            here = pl.ds(pl.multiple_of((own ^ relative) * block, 8), block)
            full_ref[index * block : (index + 1) * block, :] = wide_ref[here, :].astype(
                full_ref.dtype
            )
    share_rows = share_ref.shape[0]
    share_ref[...] = wide_ref[pl.ds(pl.multiple_of(share * share_rows, 8), share_rows), :]


def slot_rows_kernel(slot_ref, row_ref, out_ref):
    slot_total = out_ref.shape[0]
    count = slot_ref.shape[0]

    def clear(step, carry):
        for part in range(16):
            out_ref[step * 16 + part] = -1
        return carry

    lax.fori_loop(0, slot_total // 16, clear, 0)

    def fill(step, carry):
        places = [slot_ref[step * 16 + part] for part in range(16)]
        taken = [row_ref[step * 16 + part] for part in range(16)]
        for slot, row in zip(places, taken):
            out_ref[slot] = row
        return carry

    lax.fori_loop(0, count // 16, fill, 0)


def pack_kernel(slot_ref, *refs):
    factor_ref, out_ref, value_ref, taken_ref, slots_ref = refs[-5:]
    pieces = (len(refs) - 5) // 2
    step = pl.program_id(0)
    rows, lane_count = value_ref.shape

    def add_up(*refs):
        total = refs[0][...].astype(jnp.float32)
        for ref in refs[1:]:
            total = total + ref[...].astype(jnp.float32)
        value_ref[...] = total

    first = step < pl.num_programs(0) // 2
    pl.when(first)(lambda: add_up(*refs[:pieces]))
    pl.when(jnp.logical_not(first))(lambda: add_up(*refs[pieces : 2 * pieces]))
    chunk = 128
    slot_total = slots_ref.shape[0]

    @pl.when(step == 0)
    def _():
        def clear(index, carry):
            slots_ref[pl.ds(pl.multiple_of(index * chunk, chunk), chunk), :] = jnp.zeros(
                (chunk, lane_count), jnp.float32
            )
            return carry

        lax.fori_loop(0, slot_total // chunk, clear, 0)

    values = value_ref[...]
    lane = lax.broadcasted_iota(jnp.int32, values.shape, 1)
    factors = factor_ref[...]
    total = jnp.zeros(values.shape, jnp.float32)
    for tap in range(factors.shape[1]):
        offset = 1 - tap
        moved = values
        if offset:
            moved = pltpu.roll(values, (-offset) % lane_count, axis=1)
            source = lane + offset
            moved = jnp.where((source >= 0) & (source < lane_count), moved, 0.0)
        total = total + factors[:, tap : tap + 1] * moved
    taken_ref[...] = total
    base = step * rows

    def place(index, carry):
        first_row = index * 16
        places = [slot_ref[base + first_row + part] for part in range(16)]
        taken = [taken_ref[pl.ds(first_row + part, 1), :] for part in range(16)]
        for slot, row in zip(places, taken):
            slots_ref[pl.ds(slot, 1), :] = row
        return carry

    lax.fori_loop(0, rows // 16, place, 0)

    @pl.when(step == pl.num_programs(0) - 1)
    def _():
        def narrow(index, carry):
            here = pl.ds(pl.multiple_of(index * chunk, chunk), chunk)
            out_ref[here, :] = slots_ref[here, :].astype(out_ref.dtype)
            return carry

        lax.fori_loop(0, slot_total // chunk, narrow, 0)


def add_rounded(left, right):
    return (left.astype(jnp.float32) + right.astype(jnp.float32)).astype(jnp.bfloat16)


def params(**kwargs):
    return pltpu.CompilerParams(vmem_limit_bytes=VMEM_BYTES, **kwargs)


def window(
    images,
    references,
    noise_weight,
    prior_orient,
    segment_brick,
    segment_row,
    segment_kernel,
    kernel_taps,
):
    image_groups = lax.axis_size("img")
    freq_groups = lax.axis_size("freq")
    local_orients, local_freqs = references.shape[1:]
    image_count = images.shape[1]
    orient_count = local_orients * image_groups
    share_rows = orient_count // freq_groups
    half_window = orient_count // 8
    width = 2 * half_window + 1
    keep = round_up(width, 8)
    brick_count = image_groups * freq_groups

    by_neighbours = image_groups == 4
    order = (0, 1, 3, 2) if by_neighbours else None

    def across(value, offset):
        pairs = [(source, source ^ offset) for source in range(image_groups)]
        return lax.ppermute(value, "img", pairs)

    unpacked = references.astype(jnp.float32)
    half_rows = local_orients // 2
    blocks = []
    for part in range(2):
        own = (noise_weight * unpacked[part]).astype(jnp.bfloat16)
        if not by_neighbours:
            blocks.append(lax.all_gather(own, "img", axis=0, tiled=True))
            continue
        beside = across(own, 1)
        above = across(own, 2)
        blocks.append(
            (
                own,
                beside,
                above,
                across(beside[:half_rows], 2),
                across(above[half_rows:], 1),
            )
        )
    energies = jnp.sum(
        noise_weight * (unpacked[0] * unpacked[0] + unpacked[1] * unpacked[1]), axis=1
    )
    if by_neighbours:
        energies = [energies] + [across(energies, offset) for offset in (1, 2, 3)]
    else:
        energies = lax.all_gather(energies, "img", axis=0, tiled=True)

    segment_blocks = segment_row.shape[2]
    lane_count = local_freqs // segment_blocks
    local_segments = local_orients * segment_blocks
    targets = segment_brick.reshape(local_orients, segment_blocks).T.reshape(local_segments)
    voxel_rows = segment_row.reshape(local_orients, segment_blocks).T.reshape(local_segments)
    kernels = segment_kernel.reshape(local_orients, segment_blocks).T
    capacity = round_up(max(2, 5 * local_segments // (2 * brick_count)), 16)
    slot_total = brick_count * capacity
    named = (targets[:, None] == jnp.arange(brick_count, dtype=jnp.int32)[None, :]).astype(
        jnp.bfloat16
    )
    run = 128
    runs = local_segments // run
    lower = jnp.tril(jnp.ones((run, run), jnp.bfloat16))
    within = jnp.einsum(
        "ab,nbk->nak",
        lower,
        named.reshape(runs, run, brick_count),
        preferred_element_type=jnp.float32,
    )
    ahead = jnp.dot(
        jnp.tril(jnp.ones((runs, runs), jnp.bfloat16), -1),
        within[:, -1, :].astype(jnp.bfloat16),
        preferred_element_type=jnp.float32,
    )
    ranks = jnp.sum(
        named.reshape(runs, run, brick_count).astype(jnp.float32) * (within + ahead[:, None, :]),
        axis=2,
    ).reshape(local_segments)
    slots = targets * capacity + ranks.astype(jnp.int32) - 1
    slot_rows = pl.pallas_call(
        slot_rows_kernel,
        out_shape=jax.ShapeDtypeStruct((slot_total,), jnp.int32),
        in_specs=[pl.BlockSpec(memory_space=pltpu.SMEM)] * 2,
        out_specs=pl.BlockSpec(memory_space=pltpu.SMEM),
    )(slots, voxel_rows)
    arrived_rows = lax.all_to_all(
        slot_rows.reshape(brick_count, capacity), ("img", "freq"), 0, 0, tiled=True
    )
    phases = jnp.arange(kernel_taps.shape[0], dtype=jnp.int32)
    factors = jnp.dot(
        (kernels[..., None] == phases).astype(jnp.float32),
        kernel_taps,
        precision=lax.Precision.HIGHEST,
    )

    def scores_of(weights, part):
        return lax.dot_general(
            weights, images[part], contract_last, preferred_element_type=jnp.float32
        )

    cols = 256
    image_steps = (image_count // cols,)
    prior_row = prior_orient.reshape(1, image_count)
    prior_spec = pl.BlockSpec((1, cols), lambda i: (0, i))
    scalar_spec = pl.BlockSpec(memory_space=pltpu.SMEM)
    whole_spec = pl.BlockSpec((half_rows, local_freqs), lambda i: (0, 0))
    block_spec = pl.BlockSpec((local_orients, cols), lambda i: (0, i))
    keep_spec = pl.BlockSpec((keep, cols), lambda i: (0, i))
    place = jnp.stack([lax.axis_index("img"), lax.axis_index("freq")]).astype(jnp.int32)
    if by_neighbours:
        before = [
            lax.optimization_barrier(scores_of(blocks[0][index], 0))
            + (scores_of(blocks[1][index], 1) - 0.5 * energies[index][:, None])
            for index in range(3)
        ]
        opposite = jnp.concatenate(blocks[0][3:], axis=0)
        before.append(scores_of(opposite, 0) - 0.5 * energies[3][:, None])
        partial_scores = pl.pallas_call(
            functools.partial(tail_kernel, half_window),
            grid=image_steps,
            out_shape=jax.ShapeDtypeStruct((keep, image_count), jnp.float32),
            in_specs=[scalar_spec, prior_spec]
            + [block_spec] * 4
            + [pl.BlockSpec((None, cols, local_freqs), lambda i: (1, i, 0))]
            + [whole_spec] * 2,
            out_specs=keep_spec,
            scratch_shapes=[pltpu.VMEM((orient_count, cols), jnp.float32)],
            compiler_params=params(),
        )(place, prior_row, *before, images, blocks[1][3], blocks[1][4])
    else:
        complete = scores_of(blocks[0], 0) + scores_of(blocks[1], 1) - 0.5 * energies[:, None]
        partial_scores = pl.pallas_call(
            functools.partial(cut_kernel, half_window),
            grid=image_steps,
            out_shape=jax.ShapeDtypeStruct((keep, image_count), jnp.float32),
            in_specs=[prior_spec, pl.BlockSpec((orient_count, cols), lambda i: (0, i))],
            out_specs=keep_spec,
            compiler_params=params(),
        )(prior_row, complete)
    scores = lax.psum(partial_scores, "freq")
    rounded, own_rows = pl.pallas_call(
        functools.partial(spread_kernel, half_window, order),
        grid=image_steps,
        out_shape=(
            jax.ShapeDtypeStruct((orient_count, image_count), jnp.bfloat16),
            jax.ShapeDtypeStruct((share_rows, image_count), jnp.float32),
        ),
        in_specs=[scalar_spec, prior_spec, keep_spec],
        out_specs=(
            pl.BlockSpec((orient_count, cols), lambda i: (0, i)),
            pl.BlockSpec((share_rows, cols), lambda i: (0, i)),
        ),
        scratch_shapes=[pltpu.VMEM((orient_count, cols), jnp.float32)],
        compiler_params=params(),
    )(place, prior_row, scores)

    row_member = (
        arrived_rows.reshape(-1)[None, :] == jnp.arange(BROWS, dtype=jnp.int32)[:, None]
    ).astype(jnp.bfloat16)
    half_freqs = local_freqs // 2
    one, two, three = local_orients, 2 * local_orients, 3 * local_orients

    left, right = slice(0, half_freqs), slice(half_freqs, local_freqs)

    def sums(weights, part, rows, cols):
        return jnp.dot(
            weights[rows], images[part, :, cols], preferred_element_type=jnp.float32
        ).astype(jnp.bfloat16)

    def first_sends(weights, part):
        return (
            sums(weights, part, slice(one, three), left),
            sums(weights, part, slice(two, None), right),
        )

    def second_sends(weights, part, sends):
        beside = across(sends[0], 1)
        above = across(sends[1], 2)
        kept = sums(weights, part, slice(0, two), right)
        passed = (
            add_rounded(sums(weights, part, slice(three, None), left), beside[one:]),
            add_rounded(kept[one:], above[:one]),
        )
        return beside, above, kept, passed

    if by_neighbours:
        sends = first_sends(rounded, 0)
        beside, above, kept, passed = second_sends(rounded, 0, sends)
        last = across(passed[0], 2), across(passed[1], 1)
        pieces = [[sums(rounded, 0, slice(0, one), left), beside, last[0], kept, above, last[1]]]
        later = lax.optimization_barrier((rounded, *passed))[0]
        sends = first_sends(later, 1)
        pieces[0][0] = lax.optimization_barrier((pieces[0][0], *sends))[0]
        beside, above, kept, passed = second_sends(later, 1, sends)
        last = across(passed[0], 2), across(passed[1], 1)
        pieces.append([sums(later, 1, slice(0, one), left), beside, last[0], kept, above, last[1]])
    else:
        pieces = []
        for part in range(2):
            summed = lax.psum_scatter(
                sums(rounded, part, slice(None), slice(None)),
                "img",
                scatter_dimension=0,
                tiled=True,
            )
            pieces.append([summed[:, left], summed[:, right]])

    half_steps = segment_blocks // 2

    def first_half(row):
        return pl.BlockSpec((one, lane_count), lambda j: (row, jnp.minimum(j, half_steps - 1)))

    def second_half(row):
        return pl.BlockSpec((one, lane_count), lambda j: (row, jnp.maximum(j - half_steps, 0)))

    if by_neighbours:
        value_specs = [first_half(0)] * 3 + [second_half(0), second_half(1), second_half(0)]
    else:
        value_specs = [first_half(0), second_half(0)]
    volumes = []
    for part in range(2):
        pack = pl.pallas_call(
            pack_kernel,
            grid=(segment_blocks,),
            out_shape=jax.ShapeDtypeStruct((slot_total, lane_count), jnp.bfloat16),
            in_specs=[
                pl.BlockSpec(memory_space=pltpu.SMEM),
                *value_specs,
                pl.BlockSpec((None,) + factors.shape[1:], lambda j: (j, 0, 0)),
            ],
            out_specs=pl.BlockSpec((slot_total, lane_count), lambda j: (0, 0)),
            scratch_shapes=[
                pltpu.VMEM((local_orients, lane_count), jnp.float32),
                pltpu.VMEM((local_orients, lane_count), jnp.float32),
                pltpu.VMEM((slot_total, lane_count), jnp.float32),
            ],
            compiler_params=params(),
        )
        packed = pack(slots, *pieces[part], factors)
        arrived = lax.all_to_all(
            packed.reshape(brick_count, capacity, lane_count),
            ("img", "freq"),
            0,
            0,
            tiled=True,
        ).reshape(slot_total, lane_count)
        volumes.append(jnp.dot(row_member, arrived, preferred_element_type=jnp.float32))
    return own_rows, jnp.stack(volumes)[None]


def solution(mesh):
    in_specs = (
        P(None, "img", "freq"),
        P(None, "img", "freq"),
        P("freq"),
        P("img"),
        P("freq", "img", None, None),
        P("freq", "img", None),
        P("freq", "img", None),
        P(),
    )
    out_specs = (P("freq", "img"), P(("img", "freq"), None, None, None))
    return jax.shard_map(window, mesh=mesh, in_specs=in_specs, out_specs=out_specs, check_vma=False)
```

```python
import functools

import jax
import jax.numpy as jnp
from jax import lax
from jax.experimental import pallas as pl
from jax.experimental.pallas import tpu as pltpu
from jax.sharding import PartitionSpec as P

BROWS = 2000
LANES = 128

tempering = 0.5
contract_last = (((1,), (1,)), ((), ()))
VMEM_BYTES = 60 * 1024 * 1024


def round_up(value, multiple):
    return -(-value // multiple) * multiple


def window_start(prior, half_window, orient_count):
    start = prior - half_window
    return jnp.where(start < 0, start + orient_count, start)


def bits_of(count):
    bit = 1
    while bit < count:
        yield bit
        bit *= 2


def cut_windows(half_window, prior_ref, score_ref, out_ref):
    orient_count = score_ref.shape[0]
    keep = out_ref.shape[0]
    for lanes in range(0, out_ref.shape[1], LANES):
        cols = slice(lanes, lanes + LANES)
        start = window_start(prior_ref[:, cols], half_window, orient_count)
        x = score_ref[:, cols]
        for bit in reversed(list(bits_of(orient_count))):
            kept = min(orient_count, round_up(bit - 1 + keep, 8))
            if bit >= 8:
                moved = jnp.concatenate([x[bit:], x[:bit]], axis=0)
            else:
                moved = pltpu.roll(x, x.shape[0] - bit, axis=0)
            x = jnp.where((start & bit) != 0, moved[:kept], x[:kept])
        out_ref[:, cols] = x


def cut_kernel(half_window, prior_ref, score_ref, out_ref):
    cut_windows(half_window, prior_ref, score_ref, out_ref)


def tail_kernel(half_window, own_ref, prior_ref, b0_ref, b1_ref, b2_ref, b3_ref, image_ref,
                w_first_ref, w_second_ref, out_ref, score_ref):
    block = b0_ref.shape[0]
    part = w_first_ref.shape[0]
    own = own_ref[0]

    def rows_of(relative):
        return pl.multiple_of((own ^ relative) * block, 8)

    for relative, ref in enumerate((b0_ref, b1_ref, b2_ref)):
        score_ref[pl.ds(rows_of(relative), block), :] = ref[...]
    image = image_ref[...]
    for index, ref in enumerate((w_first_ref, w_second_ref)):
        here = pl.ds(pl.multiple_of(rows_of(3) + index * part, 8), part)
        score_ref[here, :] = b3_ref[index * part : (index + 1) * part, :] + lax.dot_general(
            ref[...], image, contract_last, preferred_element_type=jnp.float32
        )
    cut_windows(half_window, prior_ref, score_ref, out_ref)


def spread_kernel(half_window, order, own_ref, prior_ref, score_ref, full_ref, share_ref, wide_ref):
    orient_count = wide_ref.shape[0]
    width = 2 * half_window + 1
    own, share = own_ref[0], own_ref[1]
    for lanes in range(0, score_ref.shape[1], LANES):
        cols = slice(lanes, lanes + LANES)
        start = window_start(prior_ref[:, cols], half_window, orient_count)
        scores = score_ref[:, cols]
        place = lax.broadcasted_iota(jnp.int32, scores.shape, 0)
        logits = jnp.where(place < width, tempering * scores, -1e30)
        highest = jnp.max(logits, axis=0, keepdims=True)
        raised = jnp.exp(logits - highest)
        x = raised / jnp.sum(raised, axis=0, keepdims=True)
        for bit in bits_of(orient_count):
            grown = min(orient_count, round_up(x.shape[0] + bit, 8))
            extra = grown - x.shape[0]
            if extra:
                x = jnp.concatenate([x, jnp.zeros((extra, LANES), x.dtype)], axis=0)
            if bit >= 8:
                moved = jnp.concatenate([x[-bit:], x[:-bit]], axis=0)
            else:
                moved = pltpu.roll(x, bit, axis=0)
            x = jnp.where((start & bit) != 0, moved, x)
        wide_ref[:, cols] = x
    if order is None:
        full_ref[...] = wide_ref[...].astype(full_ref.dtype)
    else:
        block = orient_count // len(order)
        for index, relative in enumerate(order):
            here = pl.ds(pl.multiple_of((own ^ relative) * block, 8), block)
            full_ref[index * block : (index + 1) * block, :] = wide_ref[here, :].astype(
                full_ref.dtype
            )
    share_rows = share_ref.shape[0]
    share_ref[...] = wide_ref[pl.ds(pl.multiple_of(share * share_rows, 8), share_rows), :]


def slot_rows_kernel(slot_ref, row_ref, out_ref):
    slot_total = out_ref.shape[0]
    count = slot_ref.shape[0]

    def clear(step, carry):
        for part in range(16):
            out_ref[step * 16 + part] = -1
        return carry

    lax.fori_loop(0, slot_total // 16, clear, 0)

    def fill(step, carry):
        places = [slot_ref[step * 16 + part] for part in range(16)]
        taken = [row_ref[step * 16 + part] for part in range(16)]
        for slot, row in zip(places, taken):
            out_ref[slot] = row
        return carry

    lax.fori_loop(0, count // 16, fill, 0)


def pack_kernel(slot_ref, *refs):
    factor_ref, out_ref, value_ref, taken_ref, slots_ref = refs[-5:]
    pieces = (len(refs) - 5) // 2
    step = pl.program_id(0)
    group, rows, taps = factor_ref.shape
    lane_count = taken_ref.shape[1]
    chunk = 128
    slot_total = slots_ref.shape[0]

    def add_up(*parts):
        total = parts[0][...].astype(jnp.float32)
        for part in parts[1:]:
            total = total + part[...].astype(jnp.float32)
        value_ref[...] = total

    first = step < pl.num_programs(0) // 2
    pl.when(first)(lambda: add_up(*refs[:pieces]))
    pl.when(jnp.logical_not(first))(lambda: add_up(*refs[pieces : 2 * pieces]))

    @pl.when(step == 0)
    def _():
        def clear(index, carry):
            slots_ref[pl.ds(pl.multiple_of(index * chunk, chunk), chunk), :] = jnp.zeros(
                (chunk, lane_count), jnp.float32
            )
            return carry

        lax.fori_loop(0, slot_total // chunk, clear, 0)

    lane = lax.broadcasted_iota(jnp.int32, (rows, lane_count), 1)
    for block in range(group):
        values = value_ref[:, block * lane_count : (block + 1) * lane_count]
        factors = factor_ref[block]
        total = jnp.zeros(values.shape, jnp.float32)
        for tap in range(taps):
            offset = 1 - tap
            moved = values
            if offset:
                moved = pltpu.roll(values, (-offset) % lane_count, axis=1)
                source = lane + offset
                moved = jnp.where((source >= 0) & (source < lane_count), moved, 0.0)
            total = total + factors[:, tap : tap + 1] * moved
        taken_ref[block * rows : (block + 1) * rows, :] = total
    base = step * (group * rows)

    def place(index, carry):
        first_row = index * 16
        places = [slot_ref[base + first_row + part] for part in range(16)]
        taken = [taken_ref[pl.ds(first_row + part, 1), :] for part in range(16)]
        for slot, row in zip(places, taken):
            slots_ref[pl.ds(slot, 1), :] = row
        return carry

    lax.fori_loop(0, group * rows // 16, place, 0)

    @pl.when(step == pl.num_programs(0) - 1)
    def _():
        def narrow(index, carry):
            here = pl.ds(pl.multiple_of(index * chunk, chunk), chunk)
            out_ref[here, :] = slots_ref[here, :].astype(out_ref.dtype)
            return carry

        lax.fori_loop(0, slot_total // chunk, narrow, 0)


def add_rounded(left, right):
    return (left.astype(jnp.float32) + right.astype(jnp.float32)).astype(jnp.bfloat16)


def params(**kwargs):
    return pltpu.CompilerParams(vmem_limit_bytes=VMEM_BYTES, **kwargs)


def window(
    images,
    references,
    noise_weight,
    prior_orient,
    segment_brick,
    segment_row,
    segment_kernel,
    kernel_taps,
):
    image_groups = lax.axis_size("img")
    freq_groups = lax.axis_size("freq")
    local_orients, local_freqs = references.shape[1:]
    image_count = images.shape[1]
    orient_count = local_orients * image_groups
    share_rows = orient_count // freq_groups
    half_window = orient_count // 8
    width = 2 * half_window + 1
    keep = round_up(width, 8)
    brick_count = image_groups * freq_groups

    by_neighbours = image_groups == 4
    order = (0, 1, 3, 2) if by_neighbours else None

    def across(value, offset):
        pairs = [(source, source ^ offset) for source in range(image_groups)]
        return lax.ppermute(value, "img", pairs)

    half_rows = local_orients // 2
    blocks = []
    remaining = references
    for part in range(2):
        own = (noise_weight * remaining[part].astype(jnp.float32)).astype(jnp.bfloat16)
        own, remaining = lax.optimization_barrier((own, remaining))
        if not by_neighbours:
            blocks.append(lax.all_gather(own, "img", axis=0, tiled=True))
            continue
        beside = across(own, 1)
        above = across(own, 2)
        blocks.append(
            (
                own,
                beside,
                above,
                across(beside[:half_rows], 2),
                across(above[half_rows:], 1),
            )
        )
    unpacked = remaining.astype(jnp.float32)
    energies = jnp.sum(
        noise_weight * (unpacked[0] * unpacked[0] + unpacked[1] * unpacked[1]), axis=1
    )
    if by_neighbours:
        energies = [energies] + [across(energies, offset) for offset in (1, 2, 3)]
    else:
        energies = lax.all_gather(energies, "img", axis=0, tiled=True)

    segment_blocks = segment_row.shape[2]
    lane_count = local_freqs // segment_blocks
    local_segments = local_orients * segment_blocks
    targets = segment_brick.reshape(local_orients, segment_blocks).T.reshape(local_segments)
    voxel_rows = segment_row.reshape(local_orients, segment_blocks).T.reshape(local_segments)
    kernels = segment_kernel.reshape(local_orients, segment_blocks).T
    capacity = round_up(max(2, 5 * local_segments // (2 * brick_count)), 16)
    slot_total = brick_count * capacity
    named = (targets[:, None] == jnp.arange(brick_count, dtype=jnp.int32)[None, :]).astype(
        jnp.bfloat16
    )
    run = 128
    runs = local_segments // run
    lower = jnp.tril(jnp.ones((run, run), jnp.bfloat16))
    within = jnp.einsum(
        "ab,nbk->nak",
        lower,
        named.reshape(runs, run, brick_count),
        preferred_element_type=jnp.float32,
    )
    ahead = jnp.dot(
        jnp.tril(jnp.ones((runs, runs), jnp.bfloat16), -1),
        within[:, -1, :].astype(jnp.bfloat16),
        preferred_element_type=jnp.float32,
    )
    ranks = jnp.sum(
        named.reshape(runs, run, brick_count).astype(jnp.float32) * (within + ahead[:, None, :]),
        axis=2,
    ).reshape(local_segments)
    slots = targets * capacity + ranks.astype(jnp.int32) - 1
    slot_rows = pl.pallas_call(
        slot_rows_kernel,
        out_shape=jax.ShapeDtypeStruct((slot_total,), jnp.int32),
        in_specs=[pl.BlockSpec(memory_space=pltpu.SMEM)] * 2,
        out_specs=pl.BlockSpec(memory_space=pltpu.SMEM),
    )(slots, voxel_rows)
    arrived_rows = lax.all_to_all(
        slot_rows.reshape(brick_count, capacity), ("img", "freq"), 0, 0, tiled=True
    )
    phases = jnp.arange(kernel_taps.shape[0], dtype=jnp.int32)
    factors = jnp.dot(
        (kernels[..., None] == phases).astype(jnp.float32),
        kernel_taps,
        precision=lax.Precision.HIGHEST,
    )

    def scores_of(weights, part):
        return lax.dot_general(
            weights, images[part], contract_last, preferred_element_type=jnp.float32
        )

    cols = 256
    image_steps = (image_count // cols,)
    prior_row = prior_orient.reshape(1, image_count)
    prior_spec = pl.BlockSpec((1, cols), lambda i: (0, i))
    scalar_spec = pl.BlockSpec(memory_space=pltpu.SMEM)
    whole_spec = pl.BlockSpec((half_rows, local_freqs), lambda i: (0, 0))
    block_spec = pl.BlockSpec((local_orients, cols), lambda i: (0, i))
    keep_spec = pl.BlockSpec((keep, cols), lambda i: (0, i))
    place = jnp.stack([lax.axis_index("img"), lax.axis_index("freq")]).astype(jnp.int32)
    if by_neighbours:
        before = [
            lax.optimization_barrier(scores_of(blocks[0][index], 0))
            + (scores_of(blocks[1][index], 1) - 0.5 * energies[index][:, None])
            for index in range(3)
        ]
        opposite = jnp.concatenate(blocks[0][3:], axis=0)
        before.append(scores_of(opposite, 0) - 0.5 * energies[3][:, None])
        partial_scores = pl.pallas_call(
            functools.partial(tail_kernel, half_window),
            grid=image_steps,
            out_shape=jax.ShapeDtypeStruct((keep, image_count), jnp.float32),
            in_specs=[scalar_spec, prior_spec]
            + [block_spec] * 4
            + [pl.BlockSpec((None, cols, local_freqs), lambda i: (1, i, 0))]
            + [whole_spec] * 2,
            out_specs=keep_spec,
            scratch_shapes=[pltpu.VMEM((orient_count, cols), jnp.float32)],
            compiler_params=params(),
        )(place, prior_row, *before, images, blocks[1][3], blocks[1][4])
    else:
        complete = scores_of(blocks[0], 0) + scores_of(blocks[1], 1) - 0.5 * energies[:, None]
        partial_scores = pl.pallas_call(
            functools.partial(cut_kernel, half_window),
            grid=image_steps,
            out_shape=jax.ShapeDtypeStruct((keep, image_count), jnp.float32),
            in_specs=[prior_spec, pl.BlockSpec((orient_count, cols), lambda i: (0, i))],
            out_specs=keep_spec,
            compiler_params=params(),
        )(prior_row, complete)
    scores = lax.psum(partial_scores, "freq")
    rounded, own_rows = pl.pallas_call(
        functools.partial(spread_kernel, half_window, order),
        grid=image_steps,
        out_shape=(
            jax.ShapeDtypeStruct((orient_count, image_count), jnp.bfloat16),
            jax.ShapeDtypeStruct((share_rows, image_count), jnp.float32),
        ),
        in_specs=[scalar_spec, prior_spec, keep_spec],
        out_specs=(
            pl.BlockSpec((orient_count, cols), lambda i: (0, i)),
            pl.BlockSpec((share_rows, cols), lambda i: (0, i)),
        ),
        scratch_shapes=[pltpu.VMEM((orient_count, cols), jnp.float32)],
        compiler_params=params(),
    )(place, prior_row, scores)

    half_freqs = local_freqs // 2
    one, two, three = local_orients, 2 * local_orients, 3 * local_orients

    left, right = slice(0, half_freqs), slice(half_freqs, local_freqs)

    def sums(weights, part, rows, cols):
        return jnp.dot(
            weights[rows], images[part, :, cols], preferred_element_type=jnp.float32
        ).astype(jnp.bfloat16)

    def first_sends(weights, part):
        return (
            sums(weights, part, slice(one, three), left),
            sums(weights, part, slice(two, None), right),
        )

    def second_sends(weights, part, sends):
        beside = across(sends[0], 1)
        above = across(sends[1], 2)
        kept = sums(weights, part, slice(0, two), right)
        passed = (
            add_rounded(sums(weights, part, slice(three, None), left), beside[one:]),
            add_rounded(kept[one:], above[:one]),
        )
        return beside, above, kept, passed

    if by_neighbours:
        sends = first_sends(rounded, 0)
        beside, above, kept, passed = second_sends(rounded, 0, sends)
        last = across(passed[0], 2), across(passed[1], 1)
        pieces = [[sums(rounded, 0, slice(0, one), left), beside, last[0], kept, above, last[1]]]
        later = lax.optimization_barrier((rounded, *passed))[0]
        sends = first_sends(later, 1)
        pieces[0][0] = lax.optimization_barrier((pieces[0][0], *sends))[0]
        beside, above, kept, passed = second_sends(later, 1, sends)
        last = across(passed[0], 2), across(passed[1], 1)
        pieces.append([sums(later, 1, slice(0, one), left), beside, last[0], kept, above, last[1]])
    else:
        pieces = []
        for part in range(2):
            summed = lax.psum_scatter(
                sums(rounded, part, slice(None), slice(None)),
                "img",
                scatter_dimension=0,
                tiled=True,
            )
            pieces.append([summed[:, left], summed[:, right]])

    group = 4 if segment_blocks % 8 == 0 else 1
    steps = segment_blocks // group
    half_steps = steps // 2

    def first_half(row):
        return pl.BlockSpec(
            (one, group * lane_count), lambda j: (row, jnp.minimum(j, half_steps - 1))
        )

    def second_half(row):
        return pl.BlockSpec(
            (one, group * lane_count), lambda j: (row, jnp.maximum(j - half_steps, 0))
        )

    if by_neighbours:
        value_specs = [first_half(0)] * 3 + [second_half(0), second_half(1), second_half(0)]
    else:
        value_specs = [first_half(0), second_half(0)]

    def pack(part):
        return pl.pallas_call(
            pack_kernel,
            grid=(steps,),
            out_shape=jax.ShapeDtypeStruct((slot_total, lane_count), jnp.bfloat16),
            in_specs=[
                scalar_spec,
                *value_specs,
                pl.BlockSpec((group,) + factors.shape[1:], lambda j: (j, 0, 0)),
            ],
            out_specs=pl.BlockSpec((slot_total, lane_count), lambda j: (0, 0)),
            scratch_shapes=[
                pltpu.VMEM((one, group * lane_count), jnp.float32),
                pltpu.VMEM((group * one, lane_count), jnp.float32),
                pltpu.VMEM((slot_total, lane_count), jnp.float32),
            ],
            compiler_params=params(),
        )(slots, *pieces[part], factors)

    def deliver(packed):
        return lax.all_to_all(
            packed.reshape(brick_count, -1, lane_count), ("img", "freq"), 0, 0, tiled=True
        ).reshape(-1, lane_count)

    def place_rows(rows, terms):
        member = rows.reshape(-1)[None, :] == jnp.arange(BROWS, dtype=jnp.int32)[:, None]
        return jnp.dot(member.astype(jnp.bfloat16), terms, preferred_element_type=jnp.float32)

    volumes = [place_rows(arrived_rows, deliver(pack(part))) for part in range(2)]
    return own_rows, jnp.stack(volumes)[None]


def solution(mesh):
    in_specs = (
        P(None, "img", "freq"),
        P(None, "img", "freq"),
        P("freq"),
        P("img"),
        P("freq", "img", None, None),
        P("freq", "img", None),
        P("freq", "img", None),
        P(),
    )
    out_specs = (P("freq", "img"), P(("img", "freq"), None, None, None))
    return jax.shard_map(window, mesh=mesh, in_specs=in_specs, out_specs=out_specs, check_vma=False)
```
